768 devices in a mesh: dp: 12 (over z), tensor: 64 (over x, y, core).
Axes of the slice: x: 4, y: 8, z: 12, core: 2. Of those that a mesh axis runs over, the one named last changes fastest.
Arguments:
- tokens: bfloat16 [1536, 2048], P(('dp', 'tensor')), may hold values from -6 to 6
- cotangent: bfloat16 [1536, 2048], P(('dp', 'tensor')), may hold values from -6 to 6
- levels: int32 [12], replicated, may hold values from 0 to 3, as said below
- gate_weight: bfloat16 [2048, 16384], P(None, 'tensor'), may hold values from -0.125 to 0.125
- up_weight: bfloat16 [2048, 16384], P(None, 'tensor'), may hold values from -0.125 to 0.125
- down_weight: bfloat16 [16384, 2048], P('tensor'), may hold values from -0.046875 to 0.046875
Outputs:
- mixed: bfloat16 [1536, 2048], P(('dp', 'tensor'))
- input_grad: bfloat16 [1536, 2048], P(('dp', 'tensor'))
- gate_grad: bfloat16 [2048, 16384], P(None, 'tensor')
- up_grad: bfloat16 [2048, 16384], P(None, 'tensor')
- down_grad: bfloat16 [16384, 2048], P('tensor')
The draws below stay inside these ranges and needn't reach their ends.
Inputs may be any that keep to these rules, and one draw needn't show every extreme that they name: `levels`: every level from 0 to 3 is taken by at least one group in every draw.
All inputs are finite; a program needn't handle non-finite values.
Results may differ from the reference program's by a relative error of at most 0.014.
Values may be sent and summed in bfloat16 or wider, within the bound.
A program may use at most 128 MiB of HBM per device.

```python
import jax
import jax.numpy as jnp
from jax import lax

D = 2048
FF = 16384
TOK_GROUP = 128
GROUPS = 12
TOKENS = 1536


def draw_levels(key, part):
    order_key = jax.random.fold_in(key, 17)
    shuffled = jax.random.permutation(order_key, GROUPS)
    return (shuffled % 4).astype(jnp.int32)


def steps_of(rng, dims, cuts, least, high):
    def one(dim, parts):
        draws = jax.random.uniform(jax.random.fold_in(jax.random.fold_in(rng, 6), dim), (parts,), jnp.float32, least / len(cuts), high / len(cuts))
        return jnp.repeat(jnp.exp(draws), dims[dim] // parts).reshape((-1,) + (1,) * (len(dims) - dim - 1))

    factor_of = one(*cuts[0])
    for cut in cuts[1:]:
        factor_of = factor_of * one(*cut)
    return factor_of


def gaussian(rng, extent, width, reach, split=(), kind=jnp.bfloat16):
    loudness = steps_of(rng, extent, split, -0.22, 0.18) if split else 1.0
    array = jax.random.normal(rng, extent, jnp.float32) * width * loudness
    return jnp.minimum(jnp.maximum(array, -reach), reach).astype(kind)


def setup_inputs(seed: int = 0) -> dict:
    splits = jax.random.split(jax.random.key(seed), 7)
    return {
        "tokens": gaussian(splits[0], (TOKENS, D), 1.0, 6.0, ((0, 768),)),
        "cotangent": gaussian(splits[1], (TOKENS, D), 1.0, 6.0, ((0, 768),)),
        "levels": draw_levels(jax.random.fold_in(splits[6], 71), 0),
        "gate_weight": gaussian(splits[3], (D, FF), D ** -0.5, 0.125, ((1, 64),)),
        "up_weight": gaussian(splits[4], (D, FF), D ** -0.5, 0.125, ((1, 64),)),
        "down_weight": gaussian(splits[5], (FF, D), FF ** -0.5, 0.046875, ((0, 64),)),
    }


def group_pass(rows, cot_rows, gate_weight, up_weight, down_weight, prefix_width):
    gate_part = gate_weight[:, :prefix_width]
    up_part = up_weight[:, :prefix_width]
    down_part = down_weight[:prefix_width, :]
    gate_value = jnp.dot(rows, gate_part, preferred_element_type=jnp.float32)
    up_value = jnp.dot(rows, up_part, preferred_element_type=jnp.float32)
    sigmoid_gate = 1.0 / (1.0 + jnp.exp(-gate_value))
    hidden = (gate_value * sigmoid_gate * up_value).astype(jnp.bfloat16)
    mixed = jnp.dot(hidden, down_part, preferred_element_type=jnp.float32).astype(jnp.bfloat16)
    hidden_grad = jnp.dot(cot_rows, down_part.T, preferred_element_type=jnp.float32)
    gate_act = (hidden_grad * up_value * sigmoid_gate * (1.0 + gate_value * (1.0 - sigmoid_gate))).astype(jnp.bfloat16)
    up_act = (hidden_grad * gate_value * sigmoid_gate).astype(jnp.bfloat16)
    input_grad = (jnp.dot(gate_act, gate_part.T, preferred_element_type=jnp.float32)
                  + jnp.dot(up_act, up_part.T, preferred_element_type=jnp.float32)).astype(jnp.bfloat16)
    pad_cols = FF - prefix_width
    gate_part_grad = jnp.dot(rows.T, gate_act, preferred_element_type=jnp.float32).astype(jnp.bfloat16)
    up_part_grad = jnp.dot(rows.T, up_act, preferred_element_type=jnp.float32).astype(jnp.bfloat16)
    down_part_grad = jnp.dot(hidden.T, cot_rows, preferred_element_type=jnp.float32).astype(jnp.bfloat16)
    gate_full = jnp.pad(gate_part_grad.astype(jnp.float32), ((0, 0), (0, pad_cols)))
    up_full = jnp.pad(up_part_grad.astype(jnp.float32), ((0, 0), (0, pad_cols)))
    down_full = jnp.pad(down_part_grad.astype(jnp.float32), ((0, pad_cols), (0, 0)))
    return mixed, input_grad, gate_full, up_full, down_full


def reference(tokens, cotangent, levels, gate_weight, up_weight, down_weight):
    rows_all = tokens.reshape(GROUPS, TOK_GROUP, D)
    cot_all = cotangent.reshape(GROUPS, TOK_GROUP, D)

    def branch_for(level_value):
        def run(operands):
            return group_pass(operands[0], operands[1], gate_weight, up_weight, down_weight, FF // (2 ** level_value))
        return run

    branches = [branch_for(0), branch_for(1), branch_for(2), branch_for(3)]

    def one_group(totals, items):
        rows, cot_rows, level_now = items
        mixed, input_grad, gate_full, up_full, down_full = lax.switch(level_now, branches, (rows, cot_rows))
        totals = (totals[0] + gate_full, totals[1] + up_full, totals[2] + down_full)
        return totals, (mixed, input_grad)

    start_totals = (jnp.zeros((D, FF), jnp.float32), jnp.zeros((D, FF), jnp.float32), jnp.zeros((FF, D), jnp.float32))
    totals, outputs = lax.scan(one_group, start_totals, (rows_all, cot_all, levels.astype(jnp.int32)))
    mixed = outputs[0].reshape(TOKENS, D)
    input_grad = outputs[1].reshape(TOKENS, D)
    return (mixed, input_grad, totals[0].astype(jnp.bfloat16), totals[1].astype(jnp.bfloat16), totals[2].astype(jnp.bfloat16))
```

```python
import jax
import jax.numpy as jnp
from jax import lax
from jax.sharding import PartitionSpec as P

FF = 16384
GROUPS = 12
TOK_GROUP = 128


def body(tokens, cotangent, levels, gate_weight, up_weight, down_weight):
    local_units = gate_weight.shape[1]
    group_index = lax.axis_index("dp")
    tensor_index = lax.axis_index("tensor")
    all_tokens = lax.all_gather(tokens, ("dp", "tensor"), axis=0, tiled=True)
    all_cot = lax.all_gather(cotangent, ("dp", "tensor"), axis=0, tiled=True)
    prefix = jnp.right_shift(jnp.int32(FF), levels)
    unit_index = tensor_index * local_units + lax.iota(jnp.int32, local_units)
    active = (unit_index[None, :] < prefix[:, None])
    active = jnp.repeat(active, TOK_GROUP, axis=0)
    gate_value = jnp.dot(all_tokens, gate_weight, preferred_element_type=jnp.float32)
    up_value = jnp.dot(all_tokens, up_weight, preferred_element_type=jnp.float32)
    sigmoid_gate = 1.0 / (1.0 + jnp.exp(-gate_value))
    hidden = jnp.where(active, gate_value * sigmoid_gate * up_value, 0.0).astype(jnp.bfloat16)
    hidden_grad = jnp.dot(all_cot, down_weight.T, preferred_element_type=jnp.float32)
    hidden_grad = jnp.where(active, hidden_grad, 0.0)
    gate_act = (
        hidden_grad * up_value * sigmoid_gate * (1.0 + gate_value * (1.0 - sigmoid_gate))
    ).astype(jnp.bfloat16)
    up_act = (hidden_grad * gate_value * sigmoid_gate).astype(jnp.bfloat16)

    def mine(value):
        return lax.dynamic_slice_in_dim(value, group_index * TOK_GROUP, TOK_GROUP, 0)

    mixed = jnp.dot(mine(hidden), down_weight, preferred_element_type=jnp.float32)
    input_grad = jnp.dot(mine(gate_act), gate_weight.T, preferred_element_type=jnp.float32) + jnp.dot(
        mine(up_act), up_weight.T, preferred_element_type=jnp.float32
    )
    both = jnp.concatenate([mixed.astype(jnp.bfloat16), input_grad.astype(jnp.bfloat16)], axis=1)
    both = lax.psum_scatter(both, "tensor", scatter_dimension=0, tiled=True)
    width = mixed.shape[1]
    gate_out = jnp.dot(all_tokens.T, gate_act, preferred_element_type=jnp.float32).astype(jnp.bfloat16)
    up_out = jnp.dot(all_tokens.T, up_act, preferred_element_type=jnp.float32).astype(jnp.bfloat16)
    down_out = jnp.dot(hidden.T, all_cot, preferred_element_type=jnp.float32).astype(jnp.bfloat16)
    return (both[:, :width], both[:, width:], gate_out, up_out, down_out)


def solution(mesh):
    rows = P(("dp", "tensor"), None)
    columns = P(None, "tensor")
    units = P("tensor", None)
    return jax.shard_map(
        body,
        mesh=mesh,
        in_specs=(rows, rows, P(), columns, columns, units),
        out_specs=(rows, rows, columns, columns, units),
        check_vma=False,
    )
```

```python
import functools

import jax
import jax.numpy as jnp
from jax import lax
from jax.experimental import pallas as pl
from jax.experimental.pallas import tpu as pltpu
from jax.sharding import PartitionSpec as P

MESH = pl.DeviceIdType.MESH
F32 = jnp.float32
BF16 = jnp.bfloat16
LEAD = 20
PIECES = 10


def offset_of(j):
    odd = j % 2
    return (j // 2) * (1 - odd) - ((j + 1) // 2) * odd


def kernel(
    dims, tok, cot, lev, gate_w, up_w, down_w,
    mixed_out, grad_out, gu_out, down_out,
    r_tok, r_cot, stage, gath, gw, uw, dw, dwt, acc, gv, uv, hg, act, act_t,
    part, part_send, part_recv, sx, rx, syf, sy, ry,
    w_sem, p0_send, p0_recv, ring_recv, sib_recv, main_send, p1_send, rs_send, rs1_recv, rsx_recv, rsy_recv,
):
    nx, ny, nz, units, width, ff = dims
    hy, hz = ny // 2, nz // 2
    z = lax.axis_index("dp")
    t = lax.axis_index("tensor")
    x = t // (ny * 2)
    y = (t // 2) % ny
    c = t % 2
    rank = x * 2 + c
    colour = width // 2
    z_slots = (hz + 1) * ny
    y_slots = (nz // 4) * (hy + 1) * 4
    chunks = nz // 2

    def dev(zz, xx, yy, cc):
        return {"dp": zz, "tensor": (xx * ny + yy) * 2 + cc}

    copies = [
        pltpu.make_async_copy(gate_w, gw, w_sem.at[0]),
        pltpu.make_async_copy(up_w, uw, w_sem.at[1]),
        pltpu.make_async_copy(down_w, dw, w_sem.at[2]),
    ]
    for copy in copies:
        copy.start()

    barrier = pltpu.get_barrier_semaphore()
    greeted = 0
    for d in range(1, nx):
        for e in range(2):
            pl.semaphore_signal(barrier, inc=1, device_id=dev(z, (x + d) % nx, y, e), device_id_type=MESH)
            greeted += 1
    pl.semaphore_signal(barrier, inc=1, device_id=dev(z, x, y, 1 - c), device_id_type=MESH)
    greeted += 1
    for d in range(1, ny):
        pl.semaphore_signal(barrier, inc=1, device_id=dev(z, x, (y + d) % ny, c), device_id_type=MESH)
        greeted += 1
    for d in (1, nz - 1):
        pl.semaphore_signal(barrier, inc=1, device_id=dev((z + d) % nz, x, y, c), device_id_type=MESH)
        greeted += 1

    def clear(r, carry):
        acc[pl.ds(r * 8, 8), :] = jnp.zeros((8, width), F32)
        return carry

    lax.fori_loop(0, 3 * units // 8, clear, 0)
    pl.semaphore_wait(barrier, greeted)

    def p0(src, landing, which, slot, sem_slot, target):
        return pltpu.make_async_remote_copy(
            src_ref=src, dst_ref=landing.at[slot], send_sem=p0_send.at[which, sem_slot],
            recv_sem=p0_recv.at[which, slot], device_id=target, device_id_type=MESH,
        )

    for which, (src, landing) in enumerate(((tok, r_tok), (cot, r_cot))):
        pltpu.make_async_copy(src, landing.at[rank], p0_recv.at[which, rank]).start()
        for d in range(1, 2 * nx):
            other = (rank + d) % (2 * nx)
            p0(src, landing, which, rank, d, dev(z, other // 2, y, other % 2)).start()
    for which, (src, landing) in enumerate(((tok, r_tok), (cot, r_cot))):
        pltpu.make_async_copy(src, landing.at[rank], p0_recv.at[which, rank]).wait()
        for d in range(1, 2 * nx):
            other = (rank + d) % (2 * nx)
            p0(src, landing, which, other, d, dev(z, other // 2, y, other % 2)).wait_recv()
        for k in range(2 * nx):
            stage[2 * k:2 * k + 2, :] = landing[k].astype(F32)
        gath[z, y, :, which * width:(which + 1) * width] = stage[...].astype(BF16)

    def block(col, zz, yy, half):
        start = pl.multiple_of(half * width + col * colour, 128)
        return gath.at[zz, yy, :, pl.ds(start, colour)]

    def ring(col, zz, yy, target, send_sem):
        return pltpu.make_async_remote_copy(
            src_ref=block(col, zz, yy, c), dst_ref=block(col, zz, yy, c), send_sem=send_sem,
            recv_sem=ring_recv.at[col, zz, yy], device_id=target, device_id_type=MESH,
        )

    def sibling(col, zz, yy, half, send_sem):
        return pltpu.make_async_remote_copy(
            src_ref=block(col, zz, yy, half), dst_ref=block(col, zz, yy, half), send_sem=send_sem,
            recv_sem=sib_recv.at[col, zz, yy], device_id=dev(z, x, y, 1 - c), device_id_type=MESH,
        )

    z_next, z_prev = (z + 1) % nz, (z + nz - 1) % nz
    y_next, y_prev = (y + 1) % ny, (y + ny - 1) % ny
    to_z = (dev(z_next, x, y, c), dev(z_prev, x, y, c))
    to_y = (dev(z, x, y_next, c), dev(z, x, y_prev, c))

    def p1_block(stream, k):
        if stream == 0:
            return 0, z, (y + ny - k) % ny, to_y[0], hy
        if stream == 1:
            return 0, z, (y + k) % ny, to_y[1], ny - 1 - hy
        if stream == 2:
            return 1, (z + nz - k) % nz, y, to_z[0], hz
        return 1, (z + k) % nz, y, to_z[1], nz - 1 - hz

    def p1_step(k):
        for stream in range(4):
            col, zz, yy, target, last = p1_block(stream, k)

            @pl.when(k <= last)
            def _():
                ring(col, zz, yy, target, p1_send.at[stream, k]).wait_recv()
                sibling(col, zz, yy, c, p1_send.at[4 + stream, k]).start()

            @pl.when(k < last)
            def _():
                ring(col, zz, yy, target, p1_send.at[stream, k]).start()

    def p1_drain(k):
        for stream in range(4):
            col, zz, yy, target, last = p1_block(stream, k)

            @pl.when(k < last)
            def _():
                ring(col, zz, yy, target, p1_send.at[stream, k]).wait_send()

            @pl.when((k >= 1) & (k <= last))
            def _():
                sibling(col, zz, yy, c, p1_send.at[4 + stream, k]).wait_send()

    def main_block(stream, i):
        down = stream % 2
        if stream < 2:
            s, j = i // ny, i % ny
            yy = (y + offset_of(j) + ny) % ny
            zz = (z + s) % nz if down else (z + nz - s) % nz
            mine = (j >= ny // 2) if down else (j < ny // 2)
            live, half = i < z_slots, hz
            target, col = to_z[down], 0
        else:
            g, s, jj = i // ((hy + 1) * 4), (i // 4) % (hy + 1), i % 4
            zz = (z + offset_of(g * 4 + jj) + nz) % nz
            yy = (y + s) % ny if down else (y + ny - s) % ny
            mine = (jj >= 2) if down else (jj < 2)
            live, half = i < y_slots, hy
            target, col = to_y[down], 1
        arrives = live & (s >= 1) & ((s < half) | mine)
        forwards = live & ((s < half - 1) | ((s == half - 1) & mine))
        return col, zz, yy, target, arrives, forwards

    def main_slot(i):
        for stream in range(4):
            col, zz, yy, target, arrives, forwards = main_block(stream, i)

            @pl.when(arrives)
            def _():
                ring(col, zz, yy, target, main_send.at[stream, i]).wait_recv()

            @pl.when(forwards)
            def _():
                ring(col, zz, yy, target, main_send.at[stream, i]).start()

            @pl.when(arrives)
            def _():
                sibling(col, zz, yy, c, main_send.at[4 + stream, i]).start()

    def main_drain(i):
        for stream in range(4):
            col, zz, yy, target, arrives, forwards = main_block(stream, i)

            @pl.when(forwards)
            def _():
                ring(col, zz, yy, target, main_send.at[stream, i]).wait_send()

            @pl.when(arrives)
            def _():
                sibling(col, zz, yy, c, main_send.at[4 + stream, i]).wait_send()

    for stream in range(4):
        col, zz, yy, target, last = p1_block(stream, 0)
        ring(col, zz, yy, target, p1_send.at[stream, 0]).start()

    for copy in copies:
        copy.wait()
    dwt[...] = dw[...].T

    rows = ny * 16

    def groups_of(m):
        return (z + m) % nz, (z + nz - m - 1) % nz

    def pair(m, half):
        first, second = groups_of(m)
        top = gath[first, :, :, half * width:(half + 1) * width].reshape(rows, width)
        low = gath[second, :, :, half * width:(half + 1) * width].reshape(rows, width)
        return jnp.concatenate([top, low], axis=0)

    def wait_partner(m):
        def step(yy, carry):
            for zz in groups_of(m):
                @pl.when((zz != z) | (yy != y))
                def _():
                    for col in range(2):
                        sibling(col, zz, yy, 1 - c, p1_send.at[0, 0]).wait_recv()
            return carry

        lax.fori_loop(0, ny, step, 0)

    strip = rows // 2

    def gates(m):
        first, second = groups_of(m)

        def step(r, carry):
            here = pl.ds(pl.multiple_of(r * strip, strip), strip)
            group = jnp.where(r < 2, first, second)
            unit = t * units + lax.broadcasted_iota(jnp.int32, (strip, units), 1)
            live = unit < lax.shift_right_arithmetic(jnp.int32(ff), lev[group])
            gate, up = gv[here, :], uv[here, :]
            grad = jnp.where(live, hg[here, :], 0.0)
            sig = 1.0 / (1.0 + jnp.exp(-gate))
            act[here, 2 * units:3 * units] = jnp.where(live, gate * sig * up, 0.0).astype(BF16)
            act[here, 0:units] = (grad * up * sig * (1.0 + gate * (1.0 - sig))).astype(BF16)
            act[here, units:2 * units] = (grad * gate * sig).astype(BF16)
            return carry

        lax.fori_loop(0, 4, step, 0)
        for k in range(3):
            act_t[k * units:(k + 1) * units, :] = act[:, k * units:(k + 1) * units].T

    def weight_piece(m, q):
        k, side = q // 2, q % 2
        cols = slice(side * colour, (side + 1) * colour)
        first, second = groups_of(m)
        half = 1 if k == 2 else 0
        span = slice(half * width + side * colour, half * width + (side + 1) * colour)
        value = jnp.concatenate(
            [gath[first, :, :, span].reshape(rows, colour), gath[second, :, :, span].reshape(rows, colour)], axis=0
        )
        total = acc[k * units:(k + 1) * units, cols] + jnp.dot(
            act_t[k * units:(k + 1) * units, :], value, preferred_element_type=F32
        )

        @pl.when(m < chunks - 1)
        def _():
            acc[k * units:(k + 1) * units, cols] = total

        @pl.when(m == chunks - 1)
        def _():
            if k < 2:
                gu_out[k * units:(k + 1) * units, cols] = total.astype(BF16)
            else:
                down_out[:, cols] = total.astype(BF16)

    def piece(m, q):
        if q == 0:
            wait_partner(m)
            gv[...] = jnp.dot(pair(m, 0), gw[...], preferred_element_type=F32)
        elif q == 1:
            uv[...] = jnp.dot(pair(m, 0), uw[...], preferred_element_type=F32)
        elif q == 2:
            hg[...] = jnp.dot(pair(m, 1), dwt[...], preferred_element_type=F32)
        elif q == 3:
            gates(m)
        else:
            weight_piece(m, q - 4)

    def ordered(k):
        to = lax.broadcasted_iota(jnp.int32, (rows, rows), 0)
        src = lax.broadcasted_iota(jnp.int32, (rows, rows), 1)
        per_x = 2 * ny
        core, rest = to // (nx * per_x), to % (nx * per_x)
        xx, low = rest // per_x, rest % per_x
        origin = (low // 2) * (4 * nx) + xx * 4 + core * 2 + low % 2
        pick = (origin == src).astype(F32).astype(BF16)
        return jnp.dot(pick, act[0:rows, k * units:(k + 1) * units], preferred_element_type=F32).astype(BF16)

    def partner_part():
        return pltpu.make_async_remote_copy(
            src_ref=part_send, dst_ref=part_recv, send_sem=rs_send.at[0], recv_sem=rs1_recv,
            device_id=dev(z, x, y, 1 - c), device_id_type=MESH,
        )

    def x_part(d, slot):
        other = (x + d) % nx
        return pltpu.make_async_remote_copy(
            src_ref=sx.at[other], dst_ref=rx.at[slot], send_sem=rs_send.at[d],
            recv_sem=rsx_recv.at[slot], device_id=dev(z, other, y, c), device_id_type=MESH,
        )

    def y_part(d, slot):
        other = (y + d) % ny
        return pltpu.make_async_remote_copy(
            src_ref=sy.at[other], dst_ref=ry.at[slot], send_sem=rs_send.at[nx + d],
            recv_sem=rsy_recv.at[slot], device_id=dev(z, x, other, c), device_id_type=MESH,
        )

    nt = (((1,), (1,)), ((), ()))

    def outputs(i):
        @pl.when(i == LEAD + PIECES)
        def _():
            value = jnp.dot(ordered(2), dw[...], preferred_element_type=F32)
            part[:, :, 0:width] = value.reshape(2, rows // 2, width)

        @pl.when(i == LEAD + PIECES + 1)
        def _():
            value = lax.dot_general(ordered(0), gw[...], nt, preferred_element_type=F32)
            value = value + lax.dot_general(ordered(1), uw[...], nt, preferred_element_type=F32)
            part[:, :, width:2 * width] = value.reshape(2, rows // 2, width)

        @pl.when(i == LEAD + PIECES + 2)
        def _():
            part_send[...] = part[1 - c].astype(BF16)
            partner_part().start()

        @pl.when(i == LEAD + PIECES + 10)
        def _():
            partner_part().wait_recv()
            part[c] = part[c] + part_recv[...].astype(F32)
            sx[...] = part[c].astype(BF16).reshape(nx, 2 * ny, 2 * width)
            for d in range(1, nx):
                x_part(d, x).start()

        @pl.when(i == LEAD + PIECES + 20)
        def _():
            total = part[c, pl.ds(pl.multiple_of(x * 2 * ny, 2 * ny), 2 * ny), :]
            for d in range(1, nx):
                x_part(d, (x + d) % nx).wait_recv()
                total = total + rx[(x + d) % nx].astype(F32)
            for k in range(ny):
                syf[k] = total[2 * k:2 * k + 2, :]
                sy[k] = total[2 * k:2 * k + 2, :].astype(BF16)
            for d in range(1, ny):
                y_part(d, y).start()

        @pl.when(i == LEAD + PIECES + 30)
        def _():
            total = syf[y]
            for d in range(1, ny):
                y_part(d, (y + d) % ny).wait_recv()
                total = total + ry[(y + d) % ny].astype(F32)
            mixed_out[...] = total[:, 0:width].astype(BF16)
            grad_out[...] = total[:, width:2 * width].astype(BF16)

    slots = max(LEAD + PIECES * chunks, LEAD + PIECES + 31, z_slots, y_slots)

    def slot(i, carry):
        @pl.when((i % 2 == 1) & (i < 2 * max(hy, hz)))
        def _():
            p1_step((i + 1) // 2)

        main_slot(i)
        m = i // PIECES - LEAD // PIECES
        for q in range(PIECES):
            @pl.when((i % PIECES == q) & (m >= 0) & (m < chunks))
            def _():
                piece(m, q)

        outputs(i)
        return carry

    lax.fori_loop(0, slots, slot, 0)

    for which, (src, landing) in enumerate(((tok, r_tok), (cot, r_cot))):
        for d in range(1, 2 * nx):
            other = (rank + d) % (2 * nx)
            p0(src, landing, which, rank, d, dev(z, other // 2, y, other % 2)).wait_send()

    def drain_p1(k, carry):
        p1_drain(k)
        return carry

    lax.fori_loop(0, max(hy, hz) + 1, drain_p1, 0)

    def drain_main(i, carry):
        main_drain(i)
        return carry

    lax.fori_loop(0, max(z_slots, y_slots), drain_main, 0)
    partner_part().wait_send()
    for d in range(1, nx):
        x_part(d, x).wait_send()
    for d in range(1, ny):
        y_part(d, y).wait_send()


def make_body(nx, ny, nz, ff):
    def body(tokens, cotangent, levels, gate_weight, up_weight, down_weight):
        width, units = gate_weight.shape
        rows = ny * 16
        slots = max((nz // 2 + 1) * ny, (nz // 4) * (ny // 2 + 1) * 4)
        vmem = pl.BlockSpec(memory_space=pltpu.VMEM)
        hbm = pl.BlockSpec(memory_space=pl.ANY)
        dma = pltpu.SemaphoreType.DMA
        mixed, grad, gu, down = pl.pallas_call(
            functools.partial(kernel, (nx, ny, nz, units, width, ff)),
            out_shape=(
                jax.ShapeDtypeStruct((2, width), BF16),
                jax.ShapeDtypeStruct((2, width), BF16),
                jax.ShapeDtypeStruct((2 * units, width), BF16),
                jax.ShapeDtypeStruct((units, width), BF16),
            ),
            in_specs=[vmem, vmem, pl.BlockSpec(memory_space=pltpu.SMEM), hbm, hbm, hbm],
            out_specs=(vmem, vmem, vmem, vmem),
            scratch_shapes=[
                pltpu.VMEM((2 * nx, 2, width), BF16),
                pltpu.VMEM((2 * nx, 2, width), BF16),
                pltpu.VMEM((4 * nx, width), F32),
                pltpu.VMEM((nz, ny, 16, 2 * width), BF16),
                pltpu.VMEM((width, units), BF16),
                pltpu.VMEM((width, units), BF16),
                pltpu.VMEM((units, width), BF16),
                pltpu.VMEM((width, units), BF16),
                pltpu.VMEM((3 * units, width), F32),
                pltpu.VMEM((2 * rows, units), F32),
                pltpu.VMEM((2 * rows, units), F32),
                pltpu.VMEM((2 * rows, units), F32),
                pltpu.VMEM((2 * rows, 3 * units), BF16),
                pltpu.VMEM((3 * units, 2 * rows), BF16),
                pltpu.VMEM((2, rows // 2, 2 * width), F32),
                pltpu.VMEM((rows // 2, 2 * width), BF16),
                pltpu.VMEM((rows // 2, 2 * width), BF16),
                pltpu.VMEM((nx, 2 * ny, 2 * width), BF16),
                pltpu.VMEM((nx, 2 * ny, 2 * width), BF16),
                pltpu.VMEM((ny, 2, 2 * width), F32),
                pltpu.VMEM((ny, 2, 2 * width), BF16),
                pltpu.VMEM((ny, 2, 2 * width), BF16),
                dma((3,)),
                dma((2, 2 * nx)),
                dma((2, 2 * nx)),
                dma((2, nz, ny)),
                dma((2, nz, ny)),
                dma((8, slots)),
                dma((8, max(nz, ny) // 2 + 1)),
                dma((nx + ny,)),
                dma,
                dma((nx,)),
                dma((ny,)),
            ],
            compiler_params=pltpu.CompilerParams(
                collective_id=0, has_side_effects=True, vmem_limit_bytes=60 * 1024 * 1024
            ),
        )(tokens, cotangent, levels, gate_weight, up_weight, down_weight)
        return mixed, grad, gu[:units].T, gu[units:].T, down

    return body


def solution(mesh):
    rows = P(("dp", "tensor"), None)
    columns = P(None, "tensor")
    units = P("tensor", None)
    return jax.shard_map(
        make_body(4, mesh.shape["tensor"] // 8, mesh.shape["dp"], 16384),
        mesh=mesh,
        in_specs=(rows, rows, P(), columns, columns, units),
        out_specs=(rows, rows, columns, columns, units),
        check_vma=False,
    )
```

```python
import functools

import jax
import jax.numpy as jnp
from jax import lax
from jax.experimental import pallas as pl
from jax.experimental.pallas import tpu as pltpu
from jax.sharding import PartitionSpec as P

MESH = pl.DeviceIdType.MESH
F32 = jnp.float32
BF16 = jnp.bfloat16
LEAD = 6
PIECES = 7


def wrap(v, n):
    v = jnp.where(v < 0, v + n, v)
    return jnp.where(v >= n, v - n, v)


def kernel(
    dims, tok, cot, lev, gate_w, up_w, down_w,
    mixed_out, grad_out, gate_out, up_out, down_out,
    r_tok, r_cot, stage, gath, gu, dw, dwt, acc, guv, hg, act, act_t,
    part, part_send, part_recv, sx, rx, syf, sy, ry,
    w_sem, p0_send, p0_recv, ring_recv, sib_recv, sib_send, main_send, p1_send, rs_send, rs1_recv, rsx_recv, rsy_recv,
):
    nx, ny, nz, units, width, ff = dims
    hy, hz = ny // 2, nz // 2
    z = lax.axis_index("dp")
    t = lax.axis_index("tensor")
    x = t // (ny * 2)
    y = (t // 2) % ny
    c = t % 2
    rank = x * 2 + c
    colour = width // 2
    chunks = nz // 2

    def dev(zz, xx, yy, cc):
        return {"dp": zz, "tensor": (xx * ny + yy) * 2 + cc}

    copies = [
        pltpu.make_async_copy(gate_w, gu.at[:, 0:units], w_sem.at[0]),
        pltpu.make_async_copy(up_w, gu.at[:, units:2 * units], w_sem.at[1]),
        pltpu.make_async_copy(down_w, dw, w_sem.at[2]),
    ]
    for copy in copies:
        copy.start()

    barrier = pltpu.get_barrier_semaphore()
    greeted = 0
    for d in range(1, nx):
        for e in range(2):
            pl.semaphore_signal(barrier, inc=1, device_id=dev(z, wrap(x + d, nx), y, e), device_id_type=MESH)
            greeted += 1
    pl.semaphore_signal(barrier, inc=1, device_id=dev(z, x, y, 1 - c), device_id_type=MESH)
    greeted += 1
    for d in range(1, ny):
        pl.semaphore_signal(barrier, inc=1, device_id=dev(z, x, wrap(y + d, ny), c), device_id_type=MESH)
        greeted += 1
    for d in (1, nz - 1):
        pl.semaphore_signal(barrier, inc=1, device_id=dev(wrap(z + d, nz), x, y, c), device_id_type=MESH)
        greeted += 1

    def clear(r, carry):
        acc[pl.ds(r * 8, 8), :] = jnp.zeros((8, width), F32)
        return carry

    lax.fori_loop(0, 3 * units // 8, clear, 0)
    pl.semaphore_wait(barrier, greeted)

    def p0(src, landing, which, slot, sem_slot, target):
        return pltpu.make_async_remote_copy(
            src_ref=src, dst_ref=landing.at[slot], send_sem=p0_send.at[which, sem_slot],
            recv_sem=p0_recv.at[which, slot], device_id=target, device_id_type=MESH,
        )

    for which, (src, landing) in enumerate(((tok, r_tok), (cot, r_cot))):
        pltpu.make_async_copy(src, landing.at[rank], p0_recv.at[which, rank]).start()
        for d in range(1, 2 * nx):
            other = wrap(rank + d, 2 * nx)
            p0(src, landing, which, rank, d, dev(z, other // 2, y, other % 2)).start()
    for which, (src, landing) in enumerate(((tok, r_tok), (cot, r_cot))):
        pltpu.make_async_copy(src, landing.at[rank], p0_recv.at[which, rank]).wait()
        for d in range(1, 2 * nx):
            other = wrap(rank + d, 2 * nx)
            p0(src, landing, which, other, d, dev(z, other // 2, y, other % 2)).wait_recv()
        for k in range(2 * nx):
            stage[2 * k:2 * k + 2, :] = landing[k].astype(F32)
        gath[z, y, :, which * width:(which + 1) * width] = stage[...].astype(BF16)

    def block(col, zz, yy, half):
        start = pl.multiple_of(half * width + col * colour, 128)
        return gath.at[zz, yy, :, pl.ds(start, colour)]

    def ring(col, zz, yy, target, send_sem):
        return pltpu.make_async_remote_copy(
            src_ref=block(col, zz, yy, c), dst_ref=block(col, zz, yy, c), send_sem=send_sem,
            recv_sem=ring_recv.at[col, zz, yy], device_id=target, device_id_type=MESH,
        )

    def sibling(col, zz, yy, m):
        return pltpu.make_async_remote_copy(
            src_ref=block(col, zz, yy, c), dst_ref=block(col, zz, yy, c), send_sem=sib_send,
            recv_sem=sib_recv.at[m], device_id=dev(z, x, y, 1 - c), device_id_type=MESH,
        )

    z_next, z_prev = wrap(z + 1, nz), wrap(z - 1, nz)
    y_next, y_prev = wrap(y + 1, ny), wrap(y - 1, ny)
    to_z = (dev(z_next, x, y, c), dev(z_prev, x, y, c))
    to_y = (dev(z, x, y_next, c), dev(z, x, y_prev, c))

    def p1_block(stream, k):
        if stream == 0:
            return 0, z, wrap(y - k, ny), to_y[0], hy, 0
        if stream == 1:
            return 0, z, wrap(y + k, ny), to_y[1], ny - 1 - hy, 0
        if stream == 2:
            return 1, wrap(z - k, nz), y, to_z[0], hz, k - 1
        return 1, wrap(z + k, nz), y, to_z[1], nz - 1 - hz, k

    def p1_step(k):
        for stream in range(4):
            col, zz, yy, target, last, m = p1_block(stream, k)

            @pl.when(k <= last)
            def _():
                ring(col, zz, yy, target, p1_send.at[stream, k]).wait_recv()

                @pl.when(k < last)
                def _():
                    ring(col, zz, yy, target, p1_send.at[stream, k]).start()

                sibling(col, zz, yy, m).start()

    def main_slot(t, r):
        for axis in range(2):
            side, far = (hy, hz) if axis == 0 else (hz, hy)
            d, s = (r, t - r) if axis == 0 else (t - r, r)
            for e in range(2):
                live = (s >= 0) & (s <= far) & (((d >= 0) & (d <= side)) if e == 0 else ((d >= 1) & (d < side)))
                for down in range(2):
                    across = d if e else -d
                    along = s if down else -s
                    if axis == 0:
                        zz, yy, target = wrap(z + along, nz), wrap(y + across, ny), to_z[down]
                        m = s if down else s - 1
                        m = jnp.where(s == hz, chunks - 1, jnp.maximum(m, 0))
                    else:
                        zz, yy, target = wrap(z + across, nz), wrap(y + along, ny), to_y[down]
                        m = d if e else jnp.maximum(d - 1, 0)
                    if e == 1:
                        mine = down == 1
                        arrives = live & (s >= 1) & (s < far + down)
                        forwards = live & (s < far - 1 + down)
                    else:
                        mine = (d == side) if down else (d < side)
                        arrives = live & (s >= 1) & ((s < far) | mine)
                        forwards = live & ((s < far - 1) | ((s == far - 1) & mine))
                    copy = functools.partial(ring, axis, zz, yy, target, main_send.at[2 * axis + down])

                    @pl.when(arrives)
                    def _():
                        copy().wait_recv()

                    @pl.when(forwards)
                    def _():
                        copy().start()

                    @pl.when(arrives)
                    def _():
                        sibling(axis, zz, yy, m).start()

    for stream in range(4):
        col, zz, yy, target, last, m = p1_block(stream, 0)
        ring(col, zz, yy, target, p1_send.at[stream, 0]).start()

    for copy in copies:
        copy.wait()
    dwt[...] = dw[...].T

    rows = ny * 16

    def groups_of(m):
        return wrap(z + m, nz), wrap(z - m - 1, nz)

    def pair(m, half):
        first, second = groups_of(m)
        top = gath[first, :, :, half * width:(half + 1) * width].reshape(rows, width)
        low = gath[second, :, :, half * width:(half + 1) * width].reshape(rows, width)
        return jnp.concatenate([top, low], axis=0)

    def bytes_of(blocks, sem):
        span = acc.at[0:blocks * 4, :]
        return pltpu.make_async_copy(span, span, sem)

    def wait_partner(m):
        @pl.when(m == 0)
        def _():
            bytes_of(4 * ny - 2, sib_recv.at[0]).wait()

        @pl.when(m > 0)
        def _():
            bytes_of(4 * ny, sib_recv.at[m]).wait()

    strip = rows // 2

    def gates(m):
        first, second = groups_of(m)

        def step(r, carry):
            here = pl.ds(pl.multiple_of(r * strip, strip), strip)
            group = jnp.where(r < 2, first, second)
            unit = t * units + lax.broadcasted_iota(jnp.int32, (strip, units), 1)
            live = unit < lax.shift_right_arithmetic(jnp.int32(ff), lev[group])
            gate, up = guv[here, 0:units], guv[here, units:2 * units]
            grad = jnp.where(live, hg[here, :], 0.0)
            sig = 1.0 / (1.0 + jnp.exp(-gate))
            act[here, 2 * units:3 * units] = jnp.where(live, gate * sig * up, 0.0).astype(BF16)
            act[here, 0:units] = (grad * up * sig * (1.0 + gate * (1.0 - sig))).astype(BF16)
            act[here, units:2 * units] = (grad * gate * sig).astype(BF16)
            return carry

        lax.fori_loop(0, 4, step, 0)
        for k in range(3):
            act_t[k * units:(k + 1) * units, :] = act[:, k * units:(k + 1) * units].T

    def weight_piece(m, side, down):
        cols = slice(side * colour, (side + 1) * colour)
        first, second = groups_of(m)
        span = slice(down * width + side * colour, down * width + (side + 1) * colour)
        value = jnp.concatenate(
            [gath[first, :, :, span].reshape(rows, colour), gath[second, :, :, span].reshape(rows, colour)], axis=0
        )
        lines = slice(2 * units, 3 * units) if down else slice(0, 2 * units)
        total = acc[lines, cols] + jnp.dot(act_t[lines, :], value, preferred_element_type=F32)

        @pl.when(m < chunks - 1)
        def _():
            acc[lines, cols] = total

        @pl.when(m == chunks - 1)
        def _():
            if down:
                down_out[:, cols] = total.astype(BF16)
            else:
                gate_out[:, cols] = total[0:units].astype(BF16)
                up_out[:, cols] = total[units:2 * units].astype(BF16)

    def piece(m, q):
        if q == 0:
            wait_partner(m)
            guv[...] = jnp.dot(pair(m, 0), gu[...], preferred_element_type=F32)
        elif q == 1:
            hg[...] = jnp.dot(pair(m, 1), dwt[...], preferred_element_type=F32)
        elif q == 2:
            gates(m)
        else:
            weight_piece(m, (q - 3) % 2, (q - 3) // 2)

    def ordered(k):
        to = lax.broadcasted_iota(jnp.int32, (rows, rows), 0)
        src = lax.broadcasted_iota(jnp.int32, (rows, rows), 1)
        bits_x, bits_y = nx.bit_length() - 1, ny.bit_length() - 1

        def part_of(value, low, bits):
            return jnp.bitwise_and(jnp.right_shift(value, low), (1 << bits) - 1)

        row, yy = part_of(to, 0, 1), part_of(to, 1, bits_y)
        xx, core = part_of(to, 1 + bits_y, bits_x), part_of(to, 1 + bits_y + bits_x, 1)
        origin = yy * (4 * nx) + xx * 4 + core * 2 + row
        pick = (origin == src).astype(F32).astype(BF16)
        return jnp.dot(pick, act[0:rows, k * units:(k + 1) * units], preferred_element_type=F32).astype(BF16)

    def partner_part():
        return pltpu.make_async_remote_copy(
            src_ref=part_send, dst_ref=part_recv, send_sem=rs_send.at[0], recv_sem=rs1_recv,
            device_id=dev(z, x, y, 1 - c), device_id_type=MESH,
        )

    def x_part(d, slot):
        other = wrap(x + d, nx)
        return pltpu.make_async_remote_copy(
            src_ref=sx.at[other], dst_ref=rx.at[slot], send_sem=rs_send.at[d],
            recv_sem=rsx_recv.at[slot], device_id=dev(z, other, y, c), device_id_type=MESH,
        )

    def y_part(d, slot):
        other = wrap(y + d, ny)
        return pltpu.make_async_remote_copy(
            src_ref=sy.at[other], dst_ref=ry.at[slot], send_sem=rs_send.at[nx + d],
            recv_sem=rsy_recv.at[slot], device_id=dev(z, x, other, c), device_id_type=MESH,
        )

    nt = (((1,), (1,)), ((), ()))

    def outputs(t, r):
        @pl.when((t == LEAD + 1) & (r == 0))
        def _():
            value = jnp.dot(ordered(2), dw[...], preferred_element_type=F32)
            part[:, :, 0:width] = value.reshape(2, rows // 2, width)

        @pl.when((t == LEAD + 1) & (r == 1))
        def _():
            value = lax.dot_general(ordered(0), gu[:, 0:units], nt, preferred_element_type=F32)
            value = value + lax.dot_general(ordered(1), gu[:, units:2 * units], nt, preferred_element_type=F32)
            part[:, :, width:2 * width] = value.reshape(2, rows // 2, width)

        @pl.when((t == LEAD + 1) & (r == 2))
        def _():
            part_send[...] = part[1 - c].astype(BF16)
            partner_part().start()

        @pl.when((t == LEAD + 2) & (r == 3))
        def _():
            partner_part().wait_recv()
            part[c] = part[c] + part_recv[...].astype(F32)
            sx[...] = part[c].astype(BF16).reshape(nx, 2 * ny, 2 * width)
            for d in range(1, nx):
                x_part(d, x).start()

        @pl.when((t == LEAD + 4) & (r == 1))
        def _():
            total = part[c, pl.ds(pl.multiple_of(x * 2 * ny, 2 * ny), 2 * ny), :]
            for d in range(1, nx):
                x_part(d, wrap(x + d, nx)).wait_recv()
                total = total + rx[wrap(x + d, nx)].astype(F32)
            for k in range(ny):
                syf[k] = total[2 * k:2 * k + 2, :]
                sy[k] = total[2 * k:2 * k + 2, :].astype(BF16)
            for d in range(1, ny):
                y_part(d, y).start()

        @pl.when((t == LEAD + 5) & (r == 4))
        def _():
            total = syf[y]
            for d in range(1, ny):
                y_part(d, wrap(y + d, ny)).wait_recv()
                total = total + ry[wrap(y + d, ny)].astype(F32)
            mixed_out[...] = total[:, 0:width].astype(BF16)
            grad_out[...] = total[:, width:2 * width].astype(BF16)

    def wave(t, carry):
        @pl.when((t >= 1) & (t <= max(hy, hz)))
        def _():
            p1_step(t)

        def step(r, inner):
            @pl.when(r <= hy)
            def _():
                main_slot(t, r)

            m = t - LEAD
            for q in range(PIECES):
                @pl.when((r == q) & (m >= 0))
                def _():
                    piece(m, q)

            outputs(t, r)
            return inner

        lax.fori_loop(0, PIECES, step, 0)
        return carry

    lax.fori_loop(0, LEAD + chunks, wave, 0)

    for which, (src, landing) in enumerate(((tok, r_tok), (cot, r_cot))):
        for d in range(1, 2 * nx):
            other = wrap(rank + d, 2 * nx)
            p0(src, landing, which, rank, d, dev(z, other // 2, y, other % 2)).wait_send()

    def drain_p1(k, carry):
        for stream in range(4):
            col, zz, yy, target, last, m = p1_block(stream, k)

            @pl.when(k < last)
            def _():
                ring(col, zz, yy, target, p1_send.at[stream, k]).wait_send()
        return carry

    lax.fori_loop(0, max(hy, hz), drain_p1, 0)
    bytes_of(2 * (ny * nz - 1), sib_send).wait()
    for axis in range(2):
        side, far = (ny, hz) if axis == 0 else (nz, hy)
        for down in range(2):
            bytes_of(side * (far - 1) + side // 2, main_send.at[2 * axis + down]).wait()
    partner_part().wait_send()
    for d in range(1, nx):
        x_part(d, x).wait_send()
    for d in range(1, ny):
        y_part(d, y).wait_send()


def finish_kernel(mixed, grad, gate, up, down, *refs):
    outs, (mixed_v, grad_v, gate_v, up_v, down_v, gate_t, up_t, in_sem, out_sem) = refs[:5], refs[5:]
    landing = (mixed_v, grad_v, gate_v, up_v, down_v)
    leaving = (mixed_v, grad_v, gate_t, up_t, down_v)
    order = (2, 3, 4, 0, 1)
    units, width = gate_v.shape
    into = [pltpu.make_async_copy(a, b, in_sem.at[k]) for k, (a, b) in enumerate(zip((mixed, grad, gate, up, down), landing))]
    out = [pltpu.make_async_copy(a, b, out_sem.at[k]) for k, (a, b) in enumerate(zip(leaving, outs))]
    for k in order:
        into[k].start()
    for k in order:
        into[k].wait()
        if k in (2, 3):
            for b in range(width // units):
                span = slice(b * units, (b + 1) * units)
                leaving[k][span, :] = landing[k][:, span].T
        out[k].start()
    for k in order:
        out[k].wait()


def finish(mixed, grad, gate, up, down):
    units, width = gate.shape
    hbm = pl.BlockSpec(memory_space=pl.ANY)
    small, flat, tall = (2, width), (units, width), (width, units)
    return pl.pallas_call(
        finish_kernel,
        out_shape=tuple(jax.ShapeDtypeStruct(s, BF16) for s in (small, small, tall, tall, flat)),
        in_specs=[hbm] * 5,
        out_specs=(hbm,) * 5,
        scratch_shapes=[pltpu.VMEM(s, BF16) for s in (small, small, flat, flat, flat, tall, tall)]
        + [pltpu.SemaphoreType.DMA((5,)), pltpu.SemaphoreType.DMA((5,))],
    )(mixed, grad, gate, up, down)


def make_body(nx, ny, nz, ff):
    def body(tokens, cotangent, levels, gate_weight, up_weight, down_weight):
        width, units = gate_weight.shape
        rows = ny * 16
        vmem = pl.BlockSpec(memory_space=pltpu.VMEM)
        hbm = pl.BlockSpec(memory_space=pl.ANY)
        dma = pltpu.SemaphoreType.DMA
        mixed, grad, gate, up, down = pl.pallas_call(
            functools.partial(kernel, (nx, ny, nz, units, width, ff)),
            out_shape=(
                jax.ShapeDtypeStruct((2, width), BF16),
                jax.ShapeDtypeStruct((2, width), BF16),
                jax.ShapeDtypeStruct((units, width), BF16),
                jax.ShapeDtypeStruct((units, width), BF16),
                jax.ShapeDtypeStruct((units, width), BF16),
            ),
            in_specs=[vmem, vmem, pl.BlockSpec(memory_space=pltpu.SMEM), hbm, hbm, hbm],
            out_specs=(vmem, vmem, vmem, vmem, vmem),
            scratch_shapes=[
                pltpu.VMEM((2 * nx, 2, width), BF16),
                pltpu.VMEM((2 * nx, 2, width), BF16),
                pltpu.VMEM((4 * nx, width), F32),
                pltpu.VMEM((nz, ny, 16, 2 * width), BF16),
                pltpu.VMEM((width, 2 * units), BF16),
                pltpu.VMEM((units, width), BF16),
                pltpu.VMEM((width, units), BF16),
                pltpu.VMEM((3 * units, width), F32),
                pltpu.VMEM((2 * rows, 2 * units), F32),
                pltpu.VMEM((2 * rows, units), F32),
                pltpu.VMEM((2 * rows, 3 * units), BF16),
                pltpu.VMEM((3 * units, 2 * rows), BF16),
                pltpu.VMEM((2, rows // 2, 2 * width), F32),
                pltpu.VMEM((rows // 2, 2 * width), BF16),
                pltpu.VMEM((rows // 2, 2 * width), BF16),
                pltpu.VMEM((nx, 2 * ny, 2 * width), BF16),
                pltpu.VMEM((nx, 2 * ny, 2 * width), BF16),
                pltpu.VMEM((ny, 2, 2 * width), F32),
                pltpu.VMEM((ny, 2, 2 * width), BF16),
                pltpu.VMEM((ny, 2, 2 * width), BF16),
                dma((3,)),
                dma((2, 2 * nx)),
                dma((2, 2 * nx)),
                dma((2, nz, ny)),
                dma((nz // 2,)),
                dma,
                dma((4,)),
                dma((4, max(nz, ny) // 2 + 1)),
                dma((nx + ny,)),
                dma,
                dma((nx,)),
                dma((ny,)),
            ],
            compiler_params=pltpu.CompilerParams(
                collective_id=0, has_side_effects=True, vmem_limit_bytes=60 * 1024 * 1024
            ),
        )(tokens, cotangent, levels, gate_weight, up_weight, down_weight)
        return finish(mixed, grad, gate, up, down)

    return body


def solution(mesh):
    rows = P(("dp", "tensor"), None)
    columns = P(None, "tensor")
    units = P("tensor", None)
    return jax.shard_map(
        make_body(4, mesh.shape["tensor"] // 8, mesh.shape["dp"], 16384),
        mesh=mesh,
        in_specs=(rows, rows, P(), columns, columns, units),
        out_specs=(rows, rows, columns, columns, units),
        check_vma=False,
    )
```

```python
import functools

import jax
import jax.numpy as jnp
from jax import lax
from jax.experimental import pallas as pl
from jax.experimental.pallas import tpu as pltpu
from jax.sharding import PartitionSpec as P

MESH = pl.DeviceIdType.MESH
F32 = jnp.float32
BF16 = jnp.bfloat16
LEAD = 6
PIECES = 7


def wrap(v, n):
    v = jnp.where(v < 0, v + n, v)
    return jnp.where(v >= n, v - n, v)


def kernel(
    dims, tok, cot, lev, gate_w, up_w, down_w,
    mixed_out, grad_out, gate_out, up_out, down_out,
    r_tok, r_cot, stage, gath, gu, dw, dwt, acc, guv, hg, act, act_t,
    part, part_send, part_recv, sx, rx, syf, sy, ry,
    w_sem, p0_send, p0_recv, ring_recv, sib_recv, sib_send, main_send, p1_send, rs_send, rs1_recv, rsx_recv, rsy_recv,
):
    nx, ny, nz, units, width, ff = dims
    hy, hz = ny // 2, nz // 2
    z = lax.axis_index("dp")
    t = lax.axis_index("tensor")
    x = t // (ny * 2)
    y = (t // 2) % ny
    c = t % 2
    rank = x * 2 + c
    colour = width // 2
    chunks = nz // 2

    def dev(zz, xx, yy, cc):
        return {"dp": zz, "tensor": (xx * ny + yy) * 2 + cc}

    copies = [
        pltpu.make_async_copy(gate_w, gu.at[:, 0:units], w_sem.at[0]),
        pltpu.make_async_copy(up_w, gu.at[:, units:2 * units], w_sem.at[1]),
        pltpu.make_async_copy(down_w, dw, w_sem.at[2]),
    ]
    for copy in copies:
        copy.start()

    barrier = pltpu.get_barrier_semaphore()
    greeted = 0
    for d in range(1, nx):
        for e in range(2):
            pl.semaphore_signal(barrier, inc=1, device_id=dev(z, wrap(x + d, nx), y, e), device_id_type=MESH)
            greeted += 1
    pl.semaphore_signal(barrier, inc=1, device_id=dev(z, x, y, 1 - c), device_id_type=MESH)
    greeted += 1
    for d in range(1, ny):
        pl.semaphore_signal(barrier, inc=1, device_id=dev(z, x, wrap(y + d, ny), c), device_id_type=MESH)
        greeted += 1
    for d in (1, nz - 1):
        pl.semaphore_signal(barrier, inc=1, device_id=dev(wrap(z + d, nz), x, y, c), device_id_type=MESH)
        greeted += 1

    def clear(r, carry):
        acc[pl.ds(r * 8, 8), :] = jnp.zeros((8, width), F32)
        return carry

    pl.semaphore_wait(barrier, greeted)

    def p0(src, landing, which, slot, sem_slot, target):
        return pltpu.make_async_remote_copy(
            src_ref=src, dst_ref=landing.at[slot], send_sem=p0_send.at[which, sem_slot],
            recv_sem=p0_recv.at[which, slot], device_id=target, device_id_type=MESH,
        )

    for which, (src, landing) in enumerate(((tok, r_tok), (cot, r_cot))):
        pltpu.make_async_copy(src, landing.at[rank], p0_recv.at[which, rank]).start()
        for d in range(1, 2 * nx):
            other = wrap(rank + d, 2 * nx)
            p0(src, landing, which, rank, d, dev(z, other // 2, y, other % 2)).start()
    for which, (src, landing) in enumerate(((tok, r_tok), (cot, r_cot))):
        pltpu.make_async_copy(src, landing.at[rank], p0_recv.at[which, rank]).wait()
        for d in range(1, 2 * nx):
            other = wrap(rank + d, 2 * nx)
            p0(src, landing, which, other, d, dev(z, other // 2, y, other % 2)).wait_recv()
        for k in range(2 * nx):
            stage[2 * k:2 * k + 2, :] = landing[k].astype(F32)
        gath[z, y, :, which * width:(which + 1) * width] = stage[...].astype(BF16)

    def block(col, zz, yy, half):
        start = pl.multiple_of(half * width + col * colour, 128)
        return gath.at[zz, yy, :, pl.ds(start, colour)]

    def ring(col, zz, yy, target, send_sem):
        return pltpu.make_async_remote_copy(
            src_ref=block(col, zz, yy, c), dst_ref=block(col, zz, yy, c), send_sem=send_sem,
            recv_sem=ring_recv.at[col, zz, yy], device_id=target, device_id_type=MESH,
        )

    def sibling(col, zz, yy, m):
        return pltpu.make_async_remote_copy(
            src_ref=block(col, zz, yy, c), dst_ref=block(col, zz, yy, c), send_sem=sib_send,
            recv_sem=sib_recv.at[m], device_id=dev(z, x, y, 1 - c), device_id_type=MESH,
        )

    z_next, z_prev = wrap(z + 1, nz), wrap(z - 1, nz)
    y_next, y_prev = wrap(y + 1, ny), wrap(y - 1, ny)
    to_z = (dev(z_next, x, y, c), dev(z_prev, x, y, c))
    to_y = (dev(z, x, y_next, c), dev(z, x, y_prev, c))

    def p1_block(stream, k):
        if stream == 0:
            return 0, z, wrap(y - k, ny), to_y[0], hy, 0
        if stream == 1:
            return 0, z, wrap(y + k, ny), to_y[1], ny - 1 - hy, 0
        if stream == 2:
            return 1, wrap(z - k, nz), y, to_z[0], hz, k - 1
        return 1, wrap(z + k, nz), y, to_z[1], nz - 1 - hz, k

    def p1_step(k):
        for stream in range(4):
            col, zz, yy, target, last, m = p1_block(stream, k)

            @pl.when(k <= last)
            def _():
                ring(col, zz, yy, target, p1_send.at[stream, k]).wait_recv()

                @pl.when(k < last)
                def _():
                    ring(col, zz, yy, target, p1_send.at[stream, k]).start()

                sibling(col, zz, yy, m).start()

    def main_slot(t, r):
        for axis in range(2):
            side, far = (hy, hz) if axis == 0 else (hz, hy)
            d, s = (r, t - r) if axis == 0 else (t - r, r)
            for e in range(2):
                live = (s >= 0) & (s <= far) & (((d >= 0) & (d <= side)) if e == 0 else ((d >= 1) & (d < side)))
                for down in range(2):
                    across = d if e else -d
                    along = s if down else -s
                    if axis == 0:
                        zz, yy, target = wrap(z + along, nz), wrap(y + across, ny), to_z[down]
                        m = s if down else s - 1
                        m = jnp.where(s == hz, chunks - 1, jnp.maximum(m, 0))
                    else:
                        zz, yy, target = wrap(z + across, nz), wrap(y + along, ny), to_y[down]
                        m = d if e else jnp.maximum(d - 1, 0)
                    if e == 1:
                        mine = down == 1
                        arrives = live & (s >= 1) & (s < far + down)
                        forwards = live & (s < far - 1 + down)
                    else:
                        mine = (d == side) if down else (d < side)
                        arrives = live & (s >= 1) & ((s < far) | mine)
                        forwards = live & ((s < far - 1) | ((s == far - 1) & mine))
                    copy = functools.partial(ring, axis, zz, yy, target, main_send.at[2 * axis + down])

                    @pl.when(arrives)
                    def _():
                        copy().wait_recv()

                    @pl.when(forwards)
                    def _():
                        copy().start()

                    @pl.when(arrives)
                    def _():
                        sibling(axis, zz, yy, m).start()

    for stream in range(4):
        col, zz, yy, target, last, m = p1_block(stream, 0)
        ring(col, zz, yy, target, p1_send.at[stream, 0]).start()

    rows = ny * 16

    def groups_of(m):
        return wrap(z + m, nz), wrap(z - m - 1, nz)

    def pair(m, half):
        first, second = groups_of(m)
        top = gath[first, :, :, half * width:(half + 1) * width].reshape(rows, width)
        low = gath[second, :, :, half * width:(half + 1) * width].reshape(rows, width)
        return jnp.concatenate([top, low], axis=0)

    def bytes_of(blocks, sem):
        span = acc.at[0:blocks * 4, :]
        return pltpu.make_async_copy(span, span, sem)

    def wait_partner(m):
        @pl.when(m == 0)
        def _():
            bytes_of(4 * ny - 2, sib_recv.at[0]).wait()

        @pl.when(m > 0)
        def _():
            bytes_of(4 * ny, sib_recv.at[m]).wait()

    strip = rows // 2

    def gates(m):
        first, second = groups_of(m)

        def step(r, carry):
            here = pl.ds(pl.multiple_of(r * strip, strip), strip)
            group = jnp.where(r < 2, first, second)
            unit = t * units + lax.broadcasted_iota(jnp.int32, (strip, units), 1)
            live = unit < lax.shift_right_arithmetic(jnp.int32(ff), lev[group])
            gate, up = guv[here, 0:units], guv[here, units:2 * units]
            grad = jnp.where(live, hg[here, :], 0.0)
            sig = 1.0 / (1.0 + jnp.exp(-gate))
            act[here, 2 * units:3 * units] = jnp.where(live, gate * sig * up, 0.0).astype(BF16)
            act[here, 0:units] = (grad * up * sig * (1.0 + gate * (1.0 - sig))).astype(BF16)
            act[here, units:2 * units] = (grad * gate * sig).astype(BF16)
            return carry

        lax.fori_loop(0, 4, step, 0)
        for k in range(3):
            act_t[k * units:(k + 1) * units, :] = act[:, k * units:(k + 1) * units].T

    def weight_piece(m, side, down):
        cols = slice(side * colour, (side + 1) * colour)
        first, second = groups_of(m)
        span = slice(down * width + side * colour, down * width + (side + 1) * colour)

        def rows_of():
            return jnp.concatenate(
                [gath[first, :, :, span].reshape(rows, colour), gath[second, :, :, span].reshape(rows, colour)], axis=0
            )

        lines = slice(2 * units, 3 * units) if down else slice(0, 2 * units)

        @pl.when(m < chunks - 1)
        def _():
            acc[lines, cols] += jnp.dot(act_t[lines, :], rows_of(), preferred_element_type=F32)

        @pl.when(m == chunks - 1)
        def _():
            total = acc[lines, cols] + jnp.dot(act_t[lines, :], rows_of(), preferred_element_type=F32)
            if down:
                down_out[:, cols] = total.astype(BF16)
            else:
                gate_out[:, cols] = total[0:units].astype(BF16)
                up_out[:, cols] = total[units:2 * units].astype(BF16)

    def piece(m, q):
        if q == 0:
            wait_partner(m)
            guv[...] = jnp.dot(pair(m, 0), gu[...], preferred_element_type=F32)
        elif q == 1:
            hg[...] = jnp.dot(pair(m, 1), dwt[...], preferred_element_type=F32)
        elif q == 2:
            gates(m)
        else:
            weight_piece(m, (q - 3) % 2, (q - 3) // 2)

    def ordered(k):
        to = lax.broadcasted_iota(jnp.int32, (rows, rows), 0)
        src = lax.broadcasted_iota(jnp.int32, (rows, rows), 1)
        bits_x, bits_y = nx.bit_length() - 1, ny.bit_length() - 1

        def part_of(value, low, bits):
            return jnp.bitwise_and(jnp.right_shift(value, low), (1 << bits) - 1)

        row, yy = part_of(to, 0, 1), part_of(to, 1, bits_y)
        xx, core = part_of(to, 1 + bits_y, bits_x), part_of(to, 1 + bits_y + bits_x, 1)
        origin = yy * (4 * nx) + xx * 4 + core * 2 + row
        pick = (origin == src).astype(F32).astype(BF16)
        return jnp.dot(pick, act[0:rows, k * units:(k + 1) * units], preferred_element_type=F32).astype(BF16)

    def partner_part():
        return pltpu.make_async_remote_copy(
            src_ref=part_send, dst_ref=part_recv, send_sem=rs_send.at[0], recv_sem=rs1_recv,
            device_id=dev(z, x, y, 1 - c), device_id_type=MESH,
        )

    def x_part(d, slot):
        other = wrap(x + d, nx)
        return pltpu.make_async_remote_copy(
            src_ref=sx.at[other], dst_ref=rx.at[slot], send_sem=rs_send.at[d],
            recv_sem=rsx_recv.at[slot], device_id=dev(z, other, y, c), device_id_type=MESH,
        )

    def y_part(d, slot):
        other = wrap(y + d, ny)
        return pltpu.make_async_remote_copy(
            src_ref=sy.at[other], dst_ref=ry.at[slot], send_sem=rs_send.at[nx + d],
            recv_sem=rsy_recv.at[slot], device_id=dev(z, x, other, c), device_id_type=MESH,
        )

    nt = (((1,), (1,)), ((), ()))

    def outputs(t, r):
        @pl.when((t == LEAD + 1) & (r == 0))
        def _():
            value = jnp.dot(ordered(2), dw[...], preferred_element_type=F32)
            part[:, :, 0:width] = value.reshape(2, rows // 2, width)

        @pl.when((t == LEAD + 1) & (r == 1))
        def _():
            value = lax.dot_general(ordered(0), gu[:, 0:units], nt, preferred_element_type=F32)
            value = value + lax.dot_general(ordered(1), gu[:, units:2 * units], nt, preferred_element_type=F32)
            part[:, :, width:2 * width] = value.reshape(2, rows // 2, width)

        @pl.when((t == LEAD + 1) & (r == 2))
        def _():
            part_send[...] = part[1 - c].astype(BF16)
            partner_part().start()

        @pl.when((t == LEAD + 2) & (r == 3))
        def _():
            partner_part().wait_recv()
            part[c] = part[c] + part_recv[...].astype(F32)
            sx[...] = part[c].astype(BF16).reshape(nx, 2 * ny, 2 * width)
            for d in range(1, nx):
                x_part(d, x).start()

        @pl.when((t == LEAD + 4) & (r == 1))
        def _():
            total = part[c, pl.ds(pl.multiple_of(x * 2 * ny, 2 * ny), 2 * ny), :]
            for d in range(1, nx):
                x_part(d, wrap(x + d, nx)).wait_recv()
                total = total + rx[wrap(x + d, nx)].astype(F32)
            for k in range(ny):
                syf[k] = total[2 * k:2 * k + 2, :]
                sy[k] = total[2 * k:2 * k + 2, :].astype(BF16)
            for d in range(1, ny):
                y_part(d, y).start()

        @pl.when((t == LEAD + 5) & (r == 4))
        def _():
            total = syf[y]
            for d in range(1, ny):
                y_part(d, wrap(y + d, ny)).wait_recv()
                total = total + ry[wrap(y + d, ny)].astype(F32)
            mixed_out[...] = total[:, 0:width].astype(BF16)
            grad_out[...] = total[:, width:2 * width].astype(BF16)

    def wave(t, carry):
        @pl.when((t >= 1) & (t <= max(hy, hz)))
        def _():
            p1_step(t)

        def step(r, inner):
            @pl.when((r <= hy) & (t >= r) & (t - r <= hz))
            def _():
                main_slot(t, r)

            @pl.when((t == 1) & (r == hy + 1))
            def _():
                lax.fori_loop(0, 3 * units // 8, clear, 0)

            @pl.when((t == 2) & (r == hy + 1))
            def _():
                for copy in copies:
                    copy.wait()
                dwt[...] = dw[...].T

            m = t - LEAD
            for q in range(PIECES):
                @pl.when((r == q) & (m >= 0))
                def _():
                    piece(m, q)

            outputs(t, r)
            return inner

        lax.fori_loop(0, PIECES, step, 0)
        return carry

    lax.fori_loop(0, LEAD + chunks, wave, 0)

    for which, (src, landing) in enumerate(((tok, r_tok), (cot, r_cot))):
        for d in range(1, 2 * nx):
            other = wrap(rank + d, 2 * nx)
            p0(src, landing, which, rank, d, dev(z, other // 2, y, other % 2)).wait_send()

    def drain_p1(k, carry):
        for stream in range(4):
            col, zz, yy, target, last, m = p1_block(stream, k)

            @pl.when(k < last)
            def _():
                ring(col, zz, yy, target, p1_send.at[stream, k]).wait_send()
        return carry

    lax.fori_loop(0, max(hy, hz), drain_p1, 0)
    bytes_of(2 * (ny * nz - 1), sib_send).wait()
    for axis in range(2):
        side, far = (ny, hz) if axis == 0 else (nz, hy)
        for down in range(2):
            bytes_of(side * (far - 1) + side // 2, main_send.at[2 * axis + down]).wait()
    partner_part().wait_send()
    for d in range(1, nx):
        x_part(d, x).wait_send()
    for d in range(1, ny):
        y_part(d, y).wait_send()


def finish_kernel(mixed, grad, gate, up, down, *refs):
    outs, (mixed_v, grad_v, gate_v, up_v, down_v, gate_t, up_t, in_sem, out_sem) = refs[:5], refs[5:]
    landing = (mixed_v, grad_v, gate_v, up_v, down_v)
    leaving = (mixed_v, grad_v, gate_t, up_t, down_v)
    order = (2, 3, 4, 0, 1)
    units, width = gate_v.shape
    into = [pltpu.make_async_copy(a, b, in_sem.at[k]) for k, (a, b) in enumerate(zip((mixed, grad, gate, up, down), landing))]
    out = [pltpu.make_async_copy(a, b, out_sem.at[k]) for k, (a, b) in enumerate(zip(leaving, outs))]
    for k in order:
        into[k].start()
    for k in order:
        into[k].wait()
        if k in (2, 3):
            for b in range(width // units):
                span = slice(b * units, (b + 1) * units)
                leaving[k][span, :] = landing[k][:, span].T
        out[k].start()
    for k in order:
        out[k].wait()


def finish(mixed, grad, gate, up, down):
    units, width = gate.shape
    hbm = pl.BlockSpec(memory_space=pl.ANY)
    small, flat, tall = (2, width), (units, width), (width, units)
    return pl.pallas_call(
        finish_kernel,
        out_shape=tuple(jax.ShapeDtypeStruct(s, BF16) for s in (small, small, tall, tall, flat)),
        in_specs=[hbm] * 5,
        out_specs=(hbm,) * 5,
        scratch_shapes=[pltpu.VMEM(s, BF16) for s in (small, small, flat, flat, flat, tall, tall)]
        + [pltpu.SemaphoreType.DMA((5,)), pltpu.SemaphoreType.DMA((5,))],
    )(mixed, grad, gate, up, down)


def make_body(nx, ny, nz, ff):
    def body(tokens, cotangent, levels, gate_weight, up_weight, down_weight):
        width, units = gate_weight.shape
        rows = ny * 16
        vmem = pl.BlockSpec(memory_space=pltpu.VMEM)
        hbm = pl.BlockSpec(memory_space=pl.ANY)
        dma = pltpu.SemaphoreType.DMA
        mixed, grad, gate, up, down = pl.pallas_call(
            functools.partial(kernel, (nx, ny, nz, units, width, ff)),
            out_shape=(
                jax.ShapeDtypeStruct((2, width), BF16),
                jax.ShapeDtypeStruct((2, width), BF16),
                jax.ShapeDtypeStruct((units, width), BF16),
                jax.ShapeDtypeStruct((units, width), BF16),
                jax.ShapeDtypeStruct((units, width), BF16),
            ),
            in_specs=[vmem, vmem, pl.BlockSpec(memory_space=pltpu.SMEM), hbm, hbm, hbm],
            out_specs=(vmem, vmem, vmem, vmem, vmem),
            scratch_shapes=[
                pltpu.VMEM((2 * nx, 2, width), BF16),
                pltpu.VMEM((2 * nx, 2, width), BF16),
                pltpu.VMEM((4 * nx, width), F32),
                pltpu.VMEM((nz, ny, 16, 2 * width), BF16),
                pltpu.VMEM((width, 2 * units), BF16),
                pltpu.VMEM((units, width), BF16),
                pltpu.VMEM((width, units), BF16),
                pltpu.VMEM((3 * units, width), F32),
                pltpu.VMEM((2 * rows, 2 * units), F32),
                pltpu.VMEM((2 * rows, units), F32),
                pltpu.VMEM((2 * rows, 3 * units), BF16),
                pltpu.VMEM((3 * units, 2 * rows), BF16),
                pltpu.VMEM((2, rows // 2, 2 * width), F32),
                pltpu.VMEM((rows // 2, 2 * width), BF16),
                pltpu.VMEM((rows // 2, 2 * width), BF16),
                pltpu.VMEM((nx, 2 * ny, 2 * width), BF16),
                pltpu.VMEM((nx, 2 * ny, 2 * width), BF16),
                pltpu.VMEM((ny, 2, 2 * width), F32),
                pltpu.VMEM((ny, 2, 2 * width), BF16),
                pltpu.VMEM((ny, 2, 2 * width), BF16),
                dma((3,)),
                dma((2, 2 * nx)),
                dma((2, 2 * nx)),
                dma((2, nz, ny)),
                dma((nz // 2,)),
                dma,
                dma((4,)),
                dma((4, max(nz, ny) // 2 + 1)),
                dma((nx + ny,)),
                dma,
                dma((nx,)),
                dma((ny,)),
            ],
            compiler_params=pltpu.CompilerParams(
                collective_id=0, has_side_effects=True, vmem_limit_bytes=60 * 1024 * 1024
            ),
        )(tokens, cotangent, levels, gate_weight, up_weight, down_weight)
        return finish(mixed, grad, gate, up, down)

    return body


def solution(mesh):
    rows = P(("dp", "tensor"), None)
    columns = P(None, "tensor")
    units = P("tensor", None)
    return jax.shard_map(
        make_body(4, mesh.shape["tensor"] // 8, mesh.shape["dp"], 16384),
        mesh=mesh,
        in_specs=(rows, rows, P(), columns, columns, units),
        out_specs=(rows, rows, columns, columns, units),
        check_vma=False,
    )
```
